32 devices in a mesh: tok: 8 (over z, x), head: 4 (over y, core).
Axes of the slice: x: 2, y: 2, z: 4, core: 2. Of those that a mesh axis runs over, the one named last changes fastest.
Arguments:
- queries: bfloat16 [2048, 3072], P('tok', 'head'), may hold values from -96 to 96
- key_rows: bfloat16 [2048, 512], P('tok', 'head'), may hold values from -6 to 6
- value_rows: bfloat16 [2048, 512], P('tok', 'head'), may hold values from -12 to 12
- tile_mask: int32 [16, 16], P('tok'), may hold values from 0 to 1, as said below
- out_weight: bfloat16 [3072, 6144], P('head'), may hold values from -0.109375 to 0.109375
Outputs:
- mixed: bfloat16 [2048, 6144], P('tok', 'head')
The draws below stay inside these ranges and needn't reach their ends.
Inputs may be any that keep to these rules, and one draw needn't show every extreme that they name: `tile_mask`: row r keeps key tile r; every row keeps between 1 and 8 tiles, and some row keeps exactly 8.
All inputs are finite; a program needn't handle non-finite values.
Results may differ from the reference program's by a relative error of at most 0.012.
Values may be sent and summed in bfloat16 or wider, within the bound.
A program may use at most 128 MiB of HBM per device.

```python
import math
import jax
import jax.numpy as jnp
from jax import lax

D = 6144
HD = 128
QH = 24
KVH = 4
TILE = 128
TOKENS = 2048


def draw_pair(key):
    base_key = jax.random.fold_in(key, 11)
    streams = jax.random.split(base_key, 2)
    key_vals = jnp.clip(jax.random.normal(streams[0], (TOKENS, KVH * HD), jnp.float32), -6.0, 6.0)
    query_vals = jnp.clip(2.5 * jax.random.normal(streams[1], (TOKENS, QH * HD), jnp.float32), -15.0, 15.0)
    return (query_vals, key_vals)


def draw_queries(key, part):
    return draw_pair(key)[0].astype(jnp.bfloat16)


def draw_key_rows(key, part):
    return draw_pair(key)[1].astype(jnp.bfloat16)


def draw_tile_mask(key, part):
    tile_count = TOKENS // TILE
    base_key = jax.random.fold_in(key, 23)
    streams = jax.random.split(base_key, 3)
    counts = jax.random.randint(streams[0], (tile_count, 1), 1, tile_count // 2 + 1)
    full_row = jax.random.randint(streams[1], (), 0, tile_count)
    counts = jnp.where(jnp.arange(tile_count)[:, None] == full_row, tile_count // 2, counts)
    scores = jax.random.randint(streams[2], (tile_count, tile_count), 0, 65536) * tile_count + jnp.arange(tile_count)[None, :]
    diagonal = jnp.arange(tile_count)[:, None] == jnp.arange(tile_count)[None, :]
    scores = jnp.where(diagonal, -1, scores)
    ranking = jnp.argsort(jnp.argsort(scores, axis=1), axis=1)
    return (ranking < counts).astype(jnp.int32)


def steps_of(stream_key, extent, cuts, smallest, high):
    factor_of = 1.0
    for dim, shards_of in cuts:
        heights = jax.random.uniform(jax.random.fold_in(jax.random.fold_in(stream_key, 6), dim), (shards_of,), jnp.float32, smallest / len(cuts), high / len(cuts))
        factor_of = factor_of * jnp.repeat(jnp.exp(heights), extent[dim] // shards_of).reshape((-1,) + (1,) * (len(extent) - 1 - dim))
    return factor_of


def centred(rng, dims, width, limit, cuts=(), dtype=jnp.bfloat16):
    result = width * jax.random.normal(rng, dims, jnp.float32)
    if cuts:
        result = result * steps_of(rng, dims, cuts, -0.22, 0.18)
    return jnp.clip(result, -limit, limit).astype(dtype)


def setup_inputs(seed: int = 0) -> dict:
    streams_of = jax.random.split(jax.random.key(seed), 6)
    return {
        "queries": draw_queries(jax.random.fold_in(streams_of[5], 71), 0),
        "key_rows": draw_key_rows(jax.random.fold_in(streams_of[5], 71), 0),
        "value_rows": centred(streams_of[2], (TOKENS, KVH * HD), 2.0, 12.0, ((0, 8), (1, 4))),
        "tile_mask": draw_tile_mask(jax.random.fold_in(streams_of[5], 71), 0),
        "out_weight": centred(streams_of[4], (QH * HD, D), (QH * HD) ** -0.5, 0.109375, ((0, 4),)),
    }


NEGATIVE = -1e+30

def reference(queries, key_rows, value_rows, tile_mask, out_weight):
    tile_count = TOKENS // TILE
    group_size = QH // KVH
    kept_most = tile_count // 2
    score_scale = 1.0 / math.sqrt(HD)
    key_blocks = key_rows.reshape(tile_count, TILE, KVH, HD)
    value_blocks = value_rows.reshape(tile_count, TILE, KVH, HD)

    def one_tile(inputs):
        query_tile, mask_row = inputs
        ordering = jnp.argsort(1 - mask_row, stable=True)[:kept_most].astype(jnp.int32)
        kept_flags = jnp.take(mask_row, ordering) > 0
        key_chosen = jnp.take(key_blocks, ordering, axis=0).astype(jnp.float32)
        value_chosen = jnp.take(value_blocks, ordering, axis=0).astype(jnp.float32)
        query_f32 = query_tile.reshape(TILE, KVH, group_size, HD).astype(jnp.float32)
        scores = jnp.einsum('qgjd,ckgd->gjqck', query_f32, key_chosen) * score_scale
        shown = kept_flags[None, None, None, :]
        tile_max = jnp.where(shown, lax.optimization_barrier(jnp.max(scores, axis=-1)), NEGATIVE)
        prob_bf = jnp.where(shown[..., None], jnp.exp(scores - tile_max[..., None]), 0.0).astype(jnp.bfloat16)
        prob_f32 = prob_bf.astype(jnp.float32)
        tile_sums = lax.optimization_barrier(jnp.sum(prob_f32, axis=-1))
        tile_parts = jnp.einsum('gjqck,ckgd->gjqcd', prob_f32, value_chosen)
        row_max = lax.optimization_barrier(jnp.max(tile_max, axis=-1))
        tile_weight = jnp.where(shown, jnp.exp(tile_max - row_max[..., None]), 0.0)
        numerator = lax.optimization_barrier(jnp.sum(tile_weight[..., None] * tile_parts, axis=3))
        denominator = lax.optimization_barrier(jnp.sum(tile_weight * tile_sums, axis=-1))
        attended = numerator / denominator[..., None]
        return attended.transpose(2, 0, 1, 3).reshape(TILE, QH * HD).astype(jnp.bfloat16)
    attention = lax.map(one_tile, (queries.reshape(tile_count, TILE, QH * HD), tile_mask))
    attention = attention.reshape(TOKENS, QH * HD)
    return jnp.dot(attention, out_weight, preferred_element_type=jnp.float32).astype(jnp.bfloat16)
```

```python
import functools
import math

import jax
import jax.numpy as jnp
from jax import lax
from jax.experimental import pallas as pl
from jax.experimental.pallas import tpu as pltpu
from jax.sharding import PartitionSpec as P

HD = 128
TILE = 128
NEGATIVE = -1e30
MESH = pl.DeviceIdType.MESH


def kernel(
    tok_count, head_count,
    mask_ref, q_hbm, k_hbm, v_hbm, w_hbm, out_hbm,
    kbuf, vbuf, q_buf, q_t, w_buf, row_max, row_sum, acc, attn,
    a_out, a_in, y_out, y_in, c_out, c_in, own_sum, result,
    local_sem, w_sem, out_sem, ring_send, ring_recv,
    a_send, a_recv, y_send, y_recv, c_send, c_recv,
):
    heads = q_t.shape[0]
    rows = q_buf.shape[0]
    tiles = rows // TILE
    pieces, _, piece = a_out.shape
    block = pieces * piece
    half = tok_count // 2
    scale = math.log2(math.e) / math.sqrt(HD)

    tok = lax.axis_index("tok")
    head = lax.axis_index("head")
    odd = lax.rem(tok, 2)
    place = (1 - odd) * (tok // 2) + odd * (tok_count - 1 - tok // 2)

    def tok_at(position):
        p = lax.rem(position + 2 * tok_count, tok_count)
        upper = p // half
        return (1 - upper) * (2 * p) + upper * (2 * (tok_count - 1 - p) + 1)

    right, left = tok_at(place + 1), tok_at(place - 1)
    mate = head + 1 - 2 * lax.rem(head, 2)
    across = lax.rem(head + head_count // 2, head_count)
    across_mate = lax.rem(mate + head_count // 2, head_count)

    k_copy = pltpu.make_async_copy(k_hbm, kbuf.at[tok], local_sem.at[0])
    v_copy = pltpu.make_async_copy(v_hbm, vbuf.at[tok], local_sem.at[1])
    q_copy = pltpu.make_async_copy(q_hbm, q_buf, local_sem.at[2])
    k_copy.start()
    v_copy.start()
    q_copy.start()
    w_copies = []
    for role, owner in enumerate((across_mate, across, mate, head)):
        columns = pl.ds(pl.multiple_of(owner * block, 128), block)
        w_copies.append(
            pltpu.make_async_copy(w_hbm.at[:, columns], w_buf.at[role], w_sem.at[role])
        )

    barrier = pltpu.get_barrier_semaphore()
    for peer in ((right, head), (left, head), (tok, mate), (tok, across)):
        pl.semaphore_signal(barrier, inc=1, device_id=peer, device_id_type=MESH)
    pl.semaphore_wait(barrier, 4)

    def message(direction, kind, step, owner):
        buf = (kbuf, vbuf)[kind]
        return pltpu.make_async_remote_copy(
            src_ref=buf.at[owner],
            dst_ref=buf.at[owner],
            send_sem=ring_send.at[direction, kind, step],
            recv_sem=ring_recv.at[direction, kind, step],
            device_id=((right, left)[direction], head),
            device_id_type=MESH,
        )

    k_copy.wait()
    message(0, 0, 0, tok).start()
    message(1, 0, 0, tok).start()
    v_copy.wait()
    message(0, 1, 0, tok).start()
    message(1, 1, 0, tok).start()
    for copy in w_copies:
        copy.start()
    q_copy.wait()
    for j in range(heads):
        q_t[j] = q_buf[:, j * HD:(j + 1) * HD].T
    row_max[...] = jnp.full_like(row_max, NEGATIVE)
    row_sum[...] = jnp.zeros_like(row_sum)
    acc[...] = jnp.zeros_like(acc)

    def absorb(owners):
        biases, turned = [], []
        for owner in owners:
            for t in range(tiles):
                parts = []
                for r in range(tiles):
                    kept = mask_ref[r, owner * tiles + t].astype(jnp.float32)
                    parts.append(jnp.full((1, TILE), (1.0 - kept) * NEGATIVE, jnp.float32))
                biases.append(jnp.concatenate(parts, axis=1))
            turned.append(vbuf[owner].T)
        for j in range(heads):
            scores = [
                jnp.dot(kbuf[owner], q_t[j], preferred_element_type=jnp.float32)
                for owner in owners
            ]
            pieces_of = [
                s[t * TILE:(t + 1) * TILE] for s in scores for t in range(tiles)
            ]
            old_max = row_max[j]
            new_max = old_max
            for s, bias in zip(pieces_of, biases):
                new_max = jnp.maximum(
                    new_max, jnp.max(s, axis=0, keepdims=True) * scale + bias
                )
            rescale = jnp.exp2(old_max - new_max)
            probs = [
                jnp.exp2(s * scale - (new_max - bias)) for s, bias in zip(pieces_of, biases)
            ]
            total = row_sum[j] * rescale
            for p in probs:
                total = total + jnp.sum(p, axis=0, keepdims=True)
            gathered = acc[j] * rescale
            for number in range(len(owners)):
                prob = jnp.concatenate(
                    [p.astype(jnp.bfloat16) for p in probs[number * tiles:(number + 1) * tiles]],
                    axis=0,
                )
                gathered = gathered + jnp.dot(
                    turned[number], prob, preferred_element_type=jnp.float32
                )
            row_max[j] = new_max
            row_sum[j] = total
            acc[j] = gathered

    absorb((tok,))

    def ring_step(step, carry):
        from_left, from_right = tok_at(place - 1 - step), tok_at(place + 1 + step)
        more = step + 1 < half - 1
        message(0, 0, step, from_left).wait_recv()
        message(0, 0, step + 1, from_left).start()
        message(1, 0, step, from_right).wait_recv()

        @pl.when(more)
        def _():
            message(1, 0, step + 1, from_right).start()

        message(0, 1, step, from_left).wait_recv()

        @pl.when(more)
        def _():
            message(0, 1, step + 1, from_left).start()

        message(1, 1, step, from_right).wait_recv()
        message(1, 1, step + 1, from_right).start()
        absorb((from_left, from_right))
        return carry

    lax.fori_loop(0, half - 1, ring_step, 0)
    far = tok_at(place + half)
    message(0, 0, half - 1, far).wait_recv()
    message(1, 1, half - 1, far).wait_recv()
    absorb((far,))

    for j in range(heads):
        attn[:, j * HD:(j + 1) * HD] = (acc[j] / row_sum[j]).T.astype(jnp.bfloat16)

    def product(role, i):
        columns = pl.ds(pl.multiple_of(i * piece, 128), piece)
        return jnp.dot(
            attn[...], w_buf[role, :, columns], preferred_element_type=jnp.float32
        )

    def hand(out, into, send, recv, i, peer):
        return pltpu.make_async_remote_copy(
            src_ref=out.at[i], dst_ref=into.at[i], send_sem=send.at[i], recv_sem=recv.at[i],
            device_id=(tok, peer), device_id_type=MESH,
        )

    hand_a = functools.partial(hand, a_out, a_in, a_send, a_recv)
    hand_y = functools.partial(hand, y_out, y_in, y_send, y_recv)
    hand_c = functools.partial(hand, c_out, c_in, c_send, c_recv)

    w_copies[0].wait()

    @pl.loop(0, pieces)
    def _(i):
        a_out[i] = product(0, i).astype(jnp.bfloat16)
        hand_a(i, mate).start()

    w_copies[1].wait()

    @pl.loop(0, pieces)
    def _(i):
        mine = product(1, i)
        hand_a(i, mate).wait_recv()
        y_out[i] = (mine + a_in[i].astype(jnp.float32)).astype(jnp.bfloat16)
        hand_y(i, across).start()

    w_copies[2].wait()

    @pl.loop(0, pieces)
    def _(i):
        c_out[i] = product(2, i).astype(jnp.bfloat16)
        hand_c(i, mate).start()

    w_copies[3].wait()

    @pl.loop(0, pieces)
    def _(i):
        mine = product(3, i)
        hand_c(i, mate).wait_recv()
        own_sum[i] = mine + c_in[i].astype(jnp.float32)

    def store(i):
        columns = pl.ds(pl.multiple_of(i * piece, 128), piece)
        return pltpu.make_async_copy(result.at[i], out_hbm.at[:, columns], out_sem.at[i])

    @pl.loop(0, pieces)
    def _(i):
        hand_y(i, across).wait_recv()
        result[i] = (own_sum[i] + y_in[i].astype(jnp.float32)).astype(jnp.bfloat16)
        store(i).start()

    @pl.loop(0, half - 1)
    def _(step):
        for direction in range(2):
            for kind in range(2):
                message(direction, kind, step, tok).wait_send()

    message(0, 0, half - 1, tok).wait_send()
    message(1, 1, half - 1, tok).wait_send()

    @pl.loop(0, pieces)
    def _(i):
        hand_a(i, mate).wait_send()
        hand_c(i, mate).wait_send()
        hand_y(i, across).wait_send()
        store(i).wait()


def per_device(tok_count, head_count, queries, key_rows, value_rows, tile_mask, out_weight):
    rows, width = queries.shape
    heads = width // HD
    block = out_weight.shape[1] // head_count
    piece = math.gcd(block, 2 * TILE)
    pieces = block // piece
    half = tok_count // 2
    bf16, f32 = jnp.bfloat16, jnp.float32
    dma = pltpu.SemaphoreType.DMA
    part = pltpu.VMEM((pieces, rows, piece), bf16)
    anywhere = pl.BlockSpec(memory_space=pl.ANY)
    return pl.pallas_call(
        functools.partial(kernel, tok_count, head_count),
        out_shape=jax.ShapeDtypeStruct((rows, block), bf16),
        in_specs=[pl.BlockSpec(memory_space=pltpu.SMEM)] + [anywhere] * 4,
        out_specs=anywhere,
        scratch_shapes=[
            pltpu.VMEM((tok_count, rows, HD), bf16),
            pltpu.VMEM((tok_count, rows, HD), bf16),
            pltpu.VMEM((rows, width), bf16),
            pltpu.VMEM((heads, HD, rows), bf16),
            pltpu.VMEM((head_count, width, block), bf16),
            pltpu.VMEM((heads, 1, rows), f32),
            pltpu.VMEM((heads, 1, rows), f32),
            pltpu.VMEM((heads, HD, rows), f32),
            pltpu.VMEM((rows, width), bf16),
            part, part, part, part, part, part,
            pltpu.VMEM((pieces, rows, piece), f32),
            part,
            dma((3,)), dma((head_count,)), dma((pieces,)),
            dma((2, 2, half)), dma((2, 2, half)),
            dma((pieces,)), dma((pieces,)), dma((pieces,)),
            dma((pieces,)), dma((pieces,)), dma((pieces,)),
        ],
        compiler_params=pltpu.CompilerParams(collective_id=0, has_side_effects=True),
    )(tile_mask, queries, key_rows, value_rows, out_weight)


def solution(mesh):
    tok_count, head_count = mesh.shape["tok"], mesh.shape["head"]
    assert head_count == 4 and tok_count % 2 == 0
    return jax.shard_map(
        functools.partial(per_device, tok_count, head_count),
        mesh=mesh,
        in_specs=(
            P("tok", "head"),
            P("tok", "head"),
            P("tok", "head"),
            P("tok", None),
            P("head", None),
        ),
        out_specs=P("tok", "head"),
        check_vma=False,
    )
```

```python
import functools
import math

import jax
import jax.numpy as jnp
from jax import lax
from jax.experimental import pallas as pl
from jax.experimental.pallas import tpu as pltpu
from jax.sharding import PartitionSpec as P

HD = 128
TILE = 128
NEGATIVE = -1e30
MESH = pl.DeviceIdType.MESH


def kernel(
    tok_count, head_count,
    mask_ref, q_hbm, k_hbm, v_hbm, w_hbm, out_hbm,
    kbuf, vbuf, q_buf, q_t, w_buf, row_max, row_sum, acc, attn,
    a_out, a_in, y_out, y_in, c_out, c_in, own_sum, result,
    local_sem, w_sem, out_sem, ring_send, ring_recv,
    a_send, a_recv, y_send, y_recv, c_send, c_recv,
):
    heads = q_t.shape[0]
    rows = q_buf.shape[0]
    tiles = rows // TILE
    pieces, _, piece = a_out.shape
    block = pieces * piece
    half = tok_count // 2
    scale = math.log2(math.e) / math.sqrt(HD)

    tok = lax.axis_index("tok")
    head = lax.axis_index("head")
    odd = lax.rem(tok, 2)
    place = (1 - odd) * (tok // 2) + odd * (tok_count - 1 - tok // 2)

    def tok_at(position):
        p = lax.rem(position + 2 * tok_count, tok_count)
        upper = p // half
        return (1 - upper) * (2 * p) + upper * (2 * (tok_count - 1 - p) + 1)

    right, left = tok_at(place + 1), tok_at(place - 1)
    mate = head + 1 - 2 * lax.rem(head, 2)
    across = lax.rem(head + head_count // 2, head_count)
    across_mate = lax.rem(mate + head_count // 2, head_count)

    k_copy = pltpu.make_async_copy(k_hbm, kbuf.at[tok], local_sem.at[0])
    v_copy = pltpu.make_async_copy(v_hbm, vbuf.at[tok], local_sem.at[1])
    q_copy = pltpu.make_async_copy(q_hbm, q_buf, local_sem.at[2])
    k_copy.start()
    v_copy.start()
    q_copy.start()
    w_copies = []
    for role, owner in enumerate((across_mate, across, mate, head)):
        columns = pl.ds(pl.multiple_of(owner * block, 128), block)
        w_copies.append(
            pltpu.make_async_copy(w_hbm.at[:, columns], w_buf.at[role], w_sem.at[role])
        )

    barrier = pltpu.get_barrier_semaphore()
    for peer in ((right, head), (left, head), (tok, mate), (tok, across)):
        pl.semaphore_signal(barrier, inc=1, device_id=peer, device_id_type=MESH)
    pl.semaphore_wait(barrier, 4)

    def message(direction, part, step, owner):
        buf = (kbuf, vbuf)[part // 2]
        lines = pl.ds(part % 2 * (rows // 2), rows // 2)
        return pltpu.make_async_remote_copy(
            src_ref=buf.at[owner, lines],
            dst_ref=buf.at[owner, lines],
            send_sem=ring_send.at[direction, part, step],
            recv_sem=ring_recv.at[direction, part, step],
            device_id=((right, left)[direction], head),
            device_id_type=MESH,
        )

    k_copy.wait()
    for part in range(2):
        message(0, part, 0, tok).start()
        message(1, part, 0, tok).start()
    v_copy.wait()
    for part in range(2, 4):
        message(0, part, 0, tok).start()
        message(1, part, 0, tok).start()
    for copy in w_copies:
        copy.start()
    q_copy.wait()
    for j in range(heads):
        q_t[j] = q_buf[:, j * HD:(j + 1) * HD].T
    row_max[...] = jnp.full_like(row_max, NEGATIVE)
    row_sum[...] = jnp.zeros_like(row_sum)
    acc[...] = jnp.zeros_like(acc)

    def absorb(owners):
        turned = [vbuf[owner].T for owner in owners]
        biases = []
        for owner in owners:
            for t in range(tiles):
                parts = []
                for r in range(tiles):
                    kept = mask_ref[r, owner * tiles + t].astype(jnp.float32)
                    parts.append(jnp.full((1, TILE), (1.0 - kept) * NEGATIVE, jnp.float32))
                biases.append(jnp.concatenate(parts, axis=1))
        for j in range(heads):
            scores = [
                jnp.dot(kbuf[owner], q_t[j], preferred_element_type=jnp.float32)
                for owner in owners
            ]
            pieces_of = [
                s[t * TILE:(t + 1) * TILE] for s in scores for t in range(tiles)
            ]
            old_max = row_max[j]
            new_max = old_max
            for s, bias in zip(pieces_of, biases):
                new_max = jnp.maximum(
                    new_max, jnp.max(s, axis=0, keepdims=True) * scale + bias
                )
            rescale = jnp.exp2(old_max - new_max)
            probs = [
                jnp.exp2(s * scale - (new_max - bias)) for s, bias in zip(pieces_of, biases)
            ]
            total = row_sum[j] * rescale
            for p in probs:
                total = total + jnp.sum(p, axis=0, keepdims=True)
            gathered = acc[j] * rescale
            for number in range(len(owners)):
                prob = jnp.concatenate(
                    [p.astype(jnp.bfloat16) for p in probs[number * tiles:(number + 1) * tiles]],
                    axis=0,
                )
                gathered = gathered + jnp.dot(
                    turned[number], prob, preferred_element_type=jnp.float32
                )
            row_max[j] = new_max
            row_sum[j] = total
            acc[j] = gathered

    absorb((tok,))

    @pl.loop(0, half - 1)
    def _(step):
        arriving = tok_at(place - 1 - step), tok_at(place + 1 + step)
        more = step + 1 < half - 1
        for part in range(4):
            for direction in range(2):
                message(direction, part, step, arriving[direction]).wait_recv()
                onward = message(direction, part, step + 1, arriving[direction])
                if part // 2 == direction:
                    onward.start()
                else:
                    pl.when(more)(onward.start)
        absorb(arriving)

    far = tok_at(place + half)
    for part in range(2):
        message(0, part, half - 1, far).wait_recv()
        message(1, part + 2, half - 1, far).wait_recv()
    absorb((far,))

    for j in range(heads):
        attn[:, j * HD:(j + 1) * HD] = (acc[j] / row_sum[j]).T.astype(jnp.bfloat16)

    def product(role, i):
        columns = pl.ds(pl.multiple_of(i * piece, 128), piece)
        return jnp.dot(
            attn[...], w_buf[role, :, columns], preferred_element_type=jnp.float32
        )

    def hand(out, into, send, recv, i, peer):
        return pltpu.make_async_remote_copy(
            src_ref=out.at[i], dst_ref=into.at[i], send_sem=send.at[i], recv_sem=recv.at[i],
            device_id=(tok, peer), device_id_type=MESH,
        )

    hand_a = functools.partial(hand, a_out, a_in, a_send, a_recv)
    hand_y = functools.partial(hand, y_out, y_in, y_send, y_recv)
    hand_c = functools.partial(hand, c_out, c_in, c_send, c_recv)

    def give(i):
        a_out[i] = product(0, i).astype(jnp.bfloat16)
        hand_a(i, mate).start()

    def cross(i):
        mine = product(1, i)
        hand_a(i, mate).wait_recv()
        y_out[i] = (mine + a_in[i].astype(jnp.float32)).astype(jnp.bfloat16)
        hand_y(i, across).start()

    ahead = min(4, pieces)
    w_copies[0].wait()
    pl.loop(0, ahead)(give)
    w_copies[1].wait()

    @pl.loop(ahead, pieces)
    def _(i):
        cross(i - ahead)
        give(i)

    pl.loop(pieces - ahead, pieces)(cross)

    w_copies[2].wait()

    @pl.loop(0, pieces)
    def _(i):
        c_out[i] = product(2, i).astype(jnp.bfloat16)
        hand_c(i, mate).start()

    w_copies[3].wait()

    @pl.loop(0, pieces)
    def _(i):
        mine = product(3, i)
        hand_c(i, mate).wait_recv()
        own_sum[i] = mine + c_in[i].astype(jnp.float32)

    def store(i):
        columns = pl.ds(pl.multiple_of(i * piece, 128), piece)
        return pltpu.make_async_copy(result.at[i], out_hbm.at[:, columns], out_sem.at[i])

    @pl.loop(0, pieces)
    def _(i):
        hand_y(i, across).wait_recv()
        result[i] = (own_sum[i] + y_in[i].astype(jnp.float32)).astype(jnp.bfloat16)
        store(i).start()

    @pl.loop(0, half - 1)
    def _(step):
        for direction in range(2):
            for part in range(4):
                message(direction, part, step, tok).wait_send()

    for part in range(2):
        message(0, part, half - 1, tok).wait_send()
        message(1, part + 2, half - 1, tok).wait_send()

    @pl.loop(0, pieces)
    def _(i):
        hand_a(i, mate).wait_send()
        hand_c(i, mate).wait_send()
        hand_y(i, across).wait_send()
        store(i).wait()


def per_device(tok_count, head_count, queries, key_rows, value_rows, tile_mask, out_weight):
    rows, width = queries.shape
    heads = width // HD
    block = out_weight.shape[1] // head_count
    piece = math.gcd(block, 2 * TILE)
    pieces = block // piece
    half = tok_count // 2
    bf16, f32 = jnp.bfloat16, jnp.float32
    dma = pltpu.SemaphoreType.DMA
    part = pltpu.VMEM((pieces, rows, piece), bf16)
    anywhere = pl.BlockSpec(memory_space=pl.ANY)
    return pl.pallas_call(
        functools.partial(kernel, tok_count, head_count),
        out_shape=jax.ShapeDtypeStruct((rows, block), bf16),
        in_specs=[pl.BlockSpec(memory_space=pltpu.SMEM)] + [anywhere] * 4,
        out_specs=anywhere,
        scratch_shapes=[
            pltpu.VMEM((tok_count, rows, HD), bf16),
            pltpu.VMEM((tok_count, rows, HD), bf16),
            pltpu.VMEM((rows, width), bf16),
            pltpu.VMEM((heads, HD, rows), bf16),
            pltpu.VMEM((head_count, width, block), bf16),
            pltpu.VMEM((heads, 1, rows), f32),
            pltpu.VMEM((heads, 1, rows), f32),
            pltpu.VMEM((heads, HD, rows), f32),
            pltpu.VMEM((rows, width), bf16),
            part, part, part, part, part, part,
            pltpu.VMEM((pieces, rows, piece), f32),
            part,
            dma((3,)), dma((head_count,)), dma((pieces,)),
            dma((2, 4, half)), dma((2, 4, half)),
            dma((pieces,)), dma((pieces,)), dma((pieces,)),
            dma((pieces,)), dma((pieces,)), dma((pieces,)),
        ],
        compiler_params=pltpu.CompilerParams(collective_id=0, has_side_effects=True),
    )(tile_mask, queries, key_rows, value_rows, out_weight)


def solution(mesh):
    tok_count, head_count = mesh.shape["tok"], mesh.shape["head"]
    assert head_count == 4 and tok_count % 2 == 0 and tok_count >= 4
    return jax.shard_map(
        functools.partial(per_device, tok_count, head_count),
        mesh=mesh,
        in_specs=(
            P("tok", "head"),
            P("tok", "head"),
            P("tok", "head"),
            P("tok", None),
            P("head", None),
        ),
        out_specs=P("tok", "head"),
        check_vma=False,
    )
```
